32 devices in a mesh: query: 2 (over y), dom: 16 (over z, x, core).
Axes of the slice: x: 2, y: 2, z: 4, core: 2. Of those that a mesh axis runs over, the one named last changes fastest.
Arguments:
- h_in: bfloat16 [4096, 256], P('dom', 'query'), may hold values from -6 to 6
- cotangent: bfloat16 [4096, 256], P('dom', 'query'), may hold values from -6 to 6
- w_one: bfloat16 [64, 64], replicated, may hold values from -0.75 to 0.75
- w_two: bfloat16 [64, 64], replicated, may hold values from -0.75 to 0.75
- rel_one: bfloat16 [535, 64], replicated, may hold values from -3 to 3
- rel_two: bfloat16 [535, 64], replicated, may hold values from -3 to 3
- query_emb: bfloat16 [535, 64], replicated, may hold values from -6 to 6
- q_head: int32 [4], P('query'), may hold values from 0 to 4095
- q_rel: int32 [4], P('query'), may hold values from 0 to 534
- bnd_rows: int32 [1024], P('dom'), may hold values from 0 to 255
- ghost_slots: int32 [256, 16], P('dom'), may hold values from 0 to 63
- edges_in: int32 [3, 16384], P(None, 'dom'), may hold values from 0 to 535, as said below
- edges_bd: int32 [3, 16384], P(None, 'dom'), may hold values from 0 to 535, as said below
Outputs:
- grad_in: float32 [4096, 256], P('dom', 'query')
- grad_w: float32 [2, 64, 64], replicated
- grad_rel: float32 [2, 535, 64], replicated
The draws below stay inside these ranges and needn't reach their ends.
Inputs may be any that keep to these rules, and one draw needn't show every extreme that they name: `edges_in`: row 0 is a local source row, row 1 a local destination row, row 2 a relation; relation 535 marks padding, which follows all real edges in each partition's block of 1024; at least a quarter of each block is real and some partition's block has no padding. `edges_bd`: row 0 is a ghost index below 256, row 1 a local destination row, row 2 a relation; relation 535 marks padding, which follows all real edges in each partition's block of 1024; at least a quarter of each block is real and some partition's block has no padding.
All inputs are finite; a program needn't handle non-finite values.
Results may differ from the reference program's by a relative error of at most 0.0049.
The reference program's roundings to bfloat16 on the way count: a program that leaves them out, or rounds other values in their place, can miss the bound.
Values may be sent and summed in bfloat16 or wider, within the bound.
A program may use at most 64 MiB of HBM per device.

```python
import jax
import jax.numpy as jnp
from jax import lax

D = 64
NREL = 535
ENT_DEV = 256
EIN = 1024
EBD = 1024
SEND = 16
BND = 64
ENTITIES = 4096
QUERIES = 4
N_DOM = 16


def edge_block(key, per_device, source_top, salt_code):
    folded = jax.random.fold_in(key, salt_code)
    subkeys = jax.random.split(folded, 5)
    source = jax.random.randint(subkeys[0], (N_DOM, per_device), 0, source_top)
    target = jax.random.randint(subkeys[1], (N_DOM, per_device), 0, ENT_DEV)
    relation = jax.random.randint(subkeys[2], (N_DOM, per_device), 0, NREL)
    alive = jax.random.randint(subkeys[3], (N_DOM,), max(per_device // 4, 1), per_device + 1)
    filled = jax.random.randint(subkeys[4], (), 0, N_DOM)
    alive = jnp.where(jnp.arange(N_DOM) == filled, per_device, alive)
    places = jnp.arange(per_device)
    relation = jnp.where(places[None, :] < alive[:, None], relation, NREL)
    return jnp.stack([source, target, relation]).reshape(3, N_DOM * per_device).astype(jnp.int32)


def draw_edges_in(key, part):
    return edge_block(key, EIN, ENT_DEV, 11)


def draw_edges_bd(key, part):
    return edge_block(key, EBD, N_DOM * SEND, 23)


def with_ends(drawn, rng, least, high):
    shape = drawn.shape
    spot = [jax.random.randint(jax.random.fold_in(rng, axis), (), 0, shape[axis]) for axis in range(len(shape))]
    drawn = drawn.at[tuple(spot)].set(least)
    longest = shape.index(max(shape))
    spot[longest] = (spot[longest] + 1) % shape[longest]
    return drawn.at[tuple(spot)].set(high)


def steps_of(key, dims, shards, smallest, largest):
    gain = 1.0
    for axis_at, blocks in shards:
        draws = jax.random.uniform(jax.random.fold_in(jax.random.fold_in(key, 6), axis_at), (blocks,), jnp.float32, smallest / len(shards), largest / len(shards))
        gain = gain * jnp.repeat(jnp.exp(draws), dims[axis_at] // blocks).reshape((-1,) + (1,) * (len(dims) - 1 - axis_at))
    return gain


def centred(rng, shape, scale, most, pieces=(), kind=jnp.bfloat16):
    factor_of = steps_of(rng, shape, pieces, -0.22, 0.18) if pieces else 1.0
    array = jax.random.normal(rng, shape, jnp.float32) * scale * factor_of
    return jnp.minimum(jnp.maximum(array, -most), most).astype(kind)


def setup_inputs(seed: int = 0) -> dict:
    seeds = jax.random.split(jax.random.key(seed), 14)
    h_in = centred(seeds[0], (ENTITIES, QUERIES * D), 1.0, 6.0, ((0, 16), (1, 2)))
    cotangent = centred(seeds[1], (ENTITIES, QUERIES * D), 1.0, 6.0, ((0, 16), (1, 2)))
    w_one = centred(seeds[2], (D, D), D ** -0.5, 0.75)
    w_two = centred(seeds[3], (D, D), D ** -0.5, 0.75)
    rel_one = centred(seeds[4], (NREL, D), 0.5, 3.0)
    rel_two = centred(seeds[5], (NREL, D), 0.5, 3.0)
    query_emb = centred(seeds[6], (NREL, D), 1.0, 6.0)
    q_head = with_ends(jax.random.randint(seeds[7], (QUERIES,), 0, ENTITIES), jax.random.fold_in(seeds[7], 1), 0, ENTITIES - 1).astype(jnp.int32)
    q_rel = with_ends(jax.random.randint(seeds[8], (QUERIES,), 0, NREL), jax.random.fold_in(seeds[8], 1), 0, NREL - 1).astype(jnp.int32)
    bnd_rows = with_ends(jax.random.randint(seeds[9], (N_DOM * BND,), 0, ENT_DEV), jax.random.fold_in(seeds[9], 1), 0, ENT_DEV - 1).astype(jnp.int32)
    ghost_slots = with_ends(jax.random.randint(seeds[10], (N_DOM * N_DOM, SEND), 0, BND), jax.random.fold_in(seeds[10], 1), 0, BND - 1).astype(jnp.int32)
    edges_in = draw_edges_in(jax.random.fold_in(seeds[13], 71), 0)
    edges_bd = draw_edges_bd(jax.random.fold_in(seeds[13], 71), 0)
    return {"h_in": h_in, "cotangent": cotangent, "w_one": w_one, "w_two": w_two, "rel_one": rel_one, "rel_two": rel_two, "query_emb": query_emb, "q_head": q_head, "q_rel": q_rel, "bnd_rows": bnd_rows, "ghost_slots": ghost_slots, "edges_in": edges_in, "edges_bd": edges_bd}


def reference(h_in, cotangent, w_one, w_two, rel_one, rel_two, query_emb, q_head, q_rel, bnd_rows, ghost_slots, edges_in, edges_bd):
    block_in = jnp.arange(N_DOM * EIN, dtype=jnp.int32) // EIN
    block_bd = jnp.arange(N_DOM * EBD, dtype=jnp.int32) // EBD
    sources_in = block_in * ENT_DEV + edges_in[0]
    targets_in = block_in * ENT_DEV + edges_in[1]
    ghost_index = edges_bd[0]
    peer_index = ghost_index // SEND
    slot_pos = ghost_index % SEND
    slot_index = ghost_slots[block_bd * N_DOM + peer_index, slot_pos]
    sources_bd = peer_index * ENT_DEV + bnd_rows[peer_index * BND + slot_index]
    targets_bd = block_bd * ENT_DEV + edges_bd[1]
    sources = jnp.concatenate([sources_in, sources_bd]).astype(jnp.int32)
    targets = jnp.concatenate([targets_in, targets_bd]).astype(jnp.int32)
    relations = jnp.concatenate([edges_in[2], edges_bd[2]]).astype(jnp.int32)

    def rel_lookup(rel_table):
        extended = jnp.concatenate([rel_table.astype(jnp.float32), jnp.zeros((1, D), jnp.float32)], axis=0)
        return extended[relations]
    rows_one = rel_lookup(rel_one)
    rows_two = rel_lookup(rel_two)

    def forward(hidden, rel_rows, weight, boost):
        message = hidden[sources].astype(jnp.float32) * rel_rows
        summed = jax.ops.segment_sum(message, targets, num_segments=ENTITIES) + boost
        summed_b = summed.astype(jnp.bfloat16)
        mixed = jnp.dot(summed_b, weight, preferred_element_type=jnp.float32)
        center = mixed - lax.optimization_barrier(jnp.mean(mixed, axis=-1, keepdims=True))
        rstd = lax.rsqrt(lax.optimization_barrier(jnp.mean(center * center, axis=-1, keepdims=True)) + 1e-05)
        return (summed_b, center * rstd, rstd)

    def backward(upstream, hidden, rel_rows, weight, summed_b, normed, rstd):
        sigmoid_val = jax.nn.sigmoid(normed)
        dact = upstream * sigmoid_val * (1.0 + normed * (1.0 - sigmoid_val))
        dmix = rstd * (dact - lax.optimization_barrier(jnp.mean(dact, axis=-1, keepdims=True)) - normed * lax.optimization_barrier(jnp.mean(dact * normed, axis=-1, keepdims=True)))
        dmix_b = dmix.astype(jnp.bfloat16)
        wgrad = jnp.dot(summed_b.T, dmix_b, preferred_element_type=jnp.float32)
        dsum = jnp.dot(dmix_b, weight.T, preferred_element_type=jnp.float32).astype(jnp.bfloat16)
        dmessage = dsum[targets].astype(jnp.float32)
        rgrad = jax.ops.segment_sum(dmessage * hidden[sources].astype(jnp.float32), relations, num_segments=NREL + 1)[:NREL]
        dhidden = upstream + jax.ops.segment_sum(dmessage * rel_rows, sources, num_segments=ENTITIES)
        return (dhidden, wgrad, rgrad)

    def per_query(qnum):
        start = qnum * D
        first = lax.dynamic_slice_in_dim(h_in, start, D, 1)
        cot_part = lax.dynamic_slice_in_dim(cotangent, start, D, 1).astype(jnp.float32)
        boost = jnp.zeros((ENTITIES, D), jnp.float32).at[q_head[qnum]].add(query_emb[q_rel[qnum]].astype(jnp.float32))
        sum_one, norm_one, rstd_one = forward(first, rows_one, w_one, boost)
        second = (jax.nn.silu(norm_one) + first.astype(jnp.float32)).astype(jnp.bfloat16)
        sum_two, norm_two, rstd_two = forward(second, rows_two, w_two, boost)
        grad_mid, wg_two, rg_two = backward(cot_part, second, rows_two, w_two, sum_two, norm_two, rstd_two)
        grad_first, wg_one, rg_one = backward(grad_mid, first, rows_one, w_one, sum_one, norm_one, rstd_one)
        return (grad_first, jnp.stack([wg_one, wg_two]), jnp.stack([rg_one, rg_two]))
    grads_all, wgrads, rgrads = lax.map(per_query, jnp.arange(QUERIES, dtype=jnp.int32))
    grad_in = jnp.transpose(grads_all, (1, 0, 2)).reshape(ENTITIES, QUERIES * D)
    scale_w = 1.0 / jnp.sqrt(jnp.float32(ENTITIES * QUERIES))
    scale_r = jnp.sqrt(jnp.float32(NREL) / jnp.float32(N_DOM * (EIN + EBD) * QUERIES))
    return (grad_in, lax.optimization_barrier(jnp.sum(wgrads, axis=0)) * scale_w, lax.optimization_barrier(jnp.sum(rgrads, axis=0)) * scale_r)
```

```python
import functools
import math

import jax
import jax.numpy as jnp
from jax import lax
from jax.experimental import pallas as pl
from jax.experimental.pallas import tpu as pltpu
from jax.sharding import PartitionSpec as P

MESH = pl.DeviceIdType.MESH
F32 = jnp.float32
BF16 = jnp.bfloat16
CHUNK = 16


def dot_nn(a, b):
    return lax.dot_general(a, b, (((1,), (0,)), ((), ())), preferred_element_type=F32)


def dot_nt(a, b):
    return lax.dot_general(a, b, (((1,), (1,)), ((), ())), preferred_element_type=F32)


def split_hi_lo(x, axis):
    hi = x.astype(BF16)
    lo = (x - hi.astype(F32)).astype(BF16)
    return jnp.concatenate([hi, lo], axis=axis)


def onehot_into(dest, ids, col0, block):
    rows = dest.shape[0]
    count = ids.shape[1]

    def fill(i, carry):
        base = pl.multiple_of(i * block, block)
        row_ids = lax.broadcasted_iota(jnp.int32, (block, count), 0) + base
        dest[pl.ds(base, block), pl.ds(col0, count)] = jnp.where(row_ids == ids, 1.0, 0.0).astype(BF16)
        return carry

    lax.fori_loop(0, rows // block, fill, 0)


def kernel(
    n_q,
    n_d,
    scale_w,
    scale_r,
    rel_count,
    rel_rows,
    h_ref,
    cot_ref,
    w1_ref,
    w2_ref,
    relt_ref,
    qhead_ref,
    qrel_ref,
    bnd_ref,
    gs_ref,
    ein_ref,
    ebd_ref,
    gin_ref,
    gw_ref,
    grel_ref,
    rt,
    vt,
    st_in,
    st_bd,
    rel_e,
    x1,
    x2,
    req,
    out1,
    ghost1,
    out2,
    ghost2,
    ret_out2,
    ret_in2,
    ret_out1,
    ret_in1,
    red_src,
    red_in,
    red_sum,
    red_all,
    xsend,
    xrecv,
    rsend,
    rrecv,
    gsend,
    grecv,
):
    me_d = lax.axis_index("dom")
    me_q = lax.axis_index("query")
    total = n_q * n_d
    lin = me_q * n_d + me_d
    feat = w1_ref.shape[0]
    rows, wide = h_ref.shape
    queries = wide // feat
    send = ghost1.shape[0] // n_d
    e_in = ein_ref.shape[1]
    e_bd = ebd_ref.shape[1]
    half = red_all.shape[1] // CHUNK * CHUNK
    n_chunks = half // CHUNK

    barrier = pltpu.get_barrier_semaphore()

    def greet(i, carry):
        t = lax.rem(lin + i, total)
        pl.semaphore_signal(
            barrier, inc=1, device_id=(t // n_d, lax.rem(t, n_d)), device_id_type=MESH
        )
        return carry

    lax.fori_loop(1, total, greet, 0)

    def block_copy(phase, src, dst, size, i, send_to):
        peer = lax.rem(me_d + i, n_d)
        del send_to
        if size is None:
            s, d = src.at[peer], dst.at[me_d]
        else:
            s = src.at[pl.ds(pl.multiple_of(peer * size, size), size)]
            d = dst.at[pl.ds(pl.multiple_of(me_d * size, size), size)]
        return pltpu.make_async_remote_copy(
            src_ref=s,
            dst_ref=d,
            send_sem=xsend.at[phase, i],
            recv_sem=xrecv.at[phase, i],
            device_id=(me_q, peer),
            device_id_type=MESH,
        )

    def exchange_start(phase, src, dst, size):
        def go(i, carry):
            block_copy(phase, src, dst, size, i, True).start()
            return carry

        lax.fori_loop(1, n_d, go, 0)
        if size is None:
            dst[me_d] = src[me_d]
        else:
            own = pl.ds(pl.multiple_of(me_d * size, size), size)
            dst[own, :] = src[own, :]

    def exchange_wait(phase, src, dst, size):
        def go(i, carry):
            block_copy(phase, src, dst, size, i, False).wait()
            return carry

        lax.fori_loop(1, n_d, go, 0)

    def reducer(c):
        return (c * total) // n_chunks

    def rs_copy(layer, c):
        t = reducer(c)
        return t, pltpu.make_async_remote_copy(
            src_ref=red_src.at[layer, pl.ds(pl.multiple_of(c * CHUNK, CHUNK), CHUNK)],
            dst_ref=red_in.at[layer, lin],
            send_sem=rsend.at[layer, c],
            recv_sem=rrecv.at[layer, lin],
            device_id=(t // n_d, lax.rem(t, n_d)),
            device_id_type=MESH,
        )

    def rs_start(layer):
        def go(c, carry):
            t, copy = rs_copy(layer, c)

            @pl.when(t != lin)
            def _():
                copy.start()

            @pl.when(t == lin)
            def _():
                red_in[layer, lin] = red_src[
                    layer, pl.ds(pl.multiple_of(c * CHUNK, CHUNK), CHUNK), :
                ]

            return carry

        lax.fori_loop(0, n_chunks, go, 0)

    def ag_copy(layer, c, i):
        t = lax.rem(lin + i, total)
        return pltpu.make_async_remote_copy(
            src_ref=red_sum.at[layer],
            dst_ref=red_all.at[layer, pl.ds(pl.multiple_of(c * CHUNK, CHUNK), CHUNK)],
            send_sem=gsend.at[layer, i],
            recv_sem=grecv.at[layer, c],
            device_id=(t // n_d, lax.rem(t, n_d)),
            device_id_type=MESH,
        )

    def rs_finish_ag_start(layer):
        def each(c, carry):
            t, copy = rs_copy(layer, c)

            @pl.when(t != lin)
            def _():
                copy.wait_send()

            @pl.when(t == lin)
            def _():
                def take(i, acc):
                    s = lax.rem(lin + i, total)
                    pltpu.make_async_remote_copy(
                        src_ref=red_src.at[layer, pl.ds(0, CHUNK)],
                        dst_ref=red_in.at[layer, s],
                        send_sem=rsend.at[layer, 0],
                        recv_sem=rrecv.at[layer, s],
                        device_id=(s // n_d, lax.rem(s, n_d)),
                        device_id_type=MESH,
                    ).wait_recv()
                    return acc + red_in[layer, s]

                acc = lax.fori_loop(1, total, take, red_in[layer, lin])
                red_sum[layer] = acc
                red_all[layer, pl.ds(pl.multiple_of(c * CHUNK, CHUNK), CHUNK), :] = acc

                def put(i, carry2):
                    ag_copy(layer, c, i).start()
                    return carry2

                lax.fori_loop(1, total, put, 0)

            return carry

        lax.fori_loop(0, n_chunks, each, 0)

    def ag_finish(layer):
        def each(c, carry):
            t = reducer(c)

            @pl.when(t == lin)
            def _():
                def done(i, carry2):
                    ag_copy(layer, c, i).wait_send()
                    return carry2

                lax.fori_loop(1, total, done, 0)

            @pl.when(t != lin)
            def _():
                ag_copy(layer, c, 1).wait_recv()

            return carry

        lax.fori_loop(0, n_chunks, each, 0)

    def pack(layer, rg, wg):
        first = half
        rest = rel_rows - first
        red_src[layer, :, pl.ds(0, feat)] = rg[:first]
        red_src[layer, pl.ds(0, rest), pl.ds(feat, feat)] = rg[first:]
        red_src[layer, pl.ds(rest, feat), pl.ds(feat, feat)] = wg
        left = first - rest - feat
        if left:
            red_src[layer, pl.ds(rest + feat, left), pl.ds(feat, feat)] = jnp.zeros((left, feat), F32)

    def unpack(layer):
        first = half
        rest = rel_rows - first
        grel_ref[layer, pl.ds(0, first), :] = red_all[layer, :, pl.ds(0, feat)] * scale_r
        grel_ref[layer, pl.ds(first, rel_count - first), :] = (
            red_all[layer, pl.ds(0, rel_count - first), pl.ds(feat, feat)] * scale_r
        )
        gw_ref[layer] = red_all[layer, pl.ds(rest, feat), pl.ds(feat, feat)] * scale_w

    onehot_into(vt, ein_ref[1:2, :], 0, 64)
    onehot_into(vt, ebd_ref[1:2, :], e_in, 64)
    pl.semaphore_wait(barrier, total - 1)
    exchange_start(0, gs_ref, req, None)
    onehot_into(st_in, ein_ref[0:1, :], 0, 64)
    onehot_into(st_bd, ebd_ref[0:1, :], 0, 64)
    onehot_into(rt, ein_ref[2:3, :], 0, 32)
    onehot_into(rt, ebd_ref[2:3, :], e_in, 32)
    rel_e[...] = dot_nn(relt_ref[pl.ds(0, 2 * feat), :], rt[...]).astype(BF16)

    row_ids = lax.broadcasted_iota(jnp.int32, (feat, rows), 1) + me_d * rows
    lane_rel = lax.broadcasted_iota(jnp.int32, (feat, relt_ref.shape[1]), 1)
    qtab = relt_ref[pl.ds(2 * feat, feat), :].astype(F32)
    boost_parts = []
    for q in range(queries):
        vec = jnp.sum(jnp.where(lane_rel == qrel_ref[q], qtab, 0.0), axis=1, keepdims=True)
        boost_parts.append(jnp.where(row_ids == qhead_ref[q], vec, 0.0))
    boost = jnp.concatenate(boost_parts, axis=0)

    exchange_wait(0, gs_ref, req, None)
    per = 128 // send
    lane_group = lax.broadcasted_iota(jnp.int32, (1, 128), 1) // send
    wanted = []
    for j in range(n_d // per):
        vec = jnp.zeros((1, 128), jnp.int32)
        for k in range(per):
            vec = jnp.where(lane_group == k, req[j * per + k, 0:1, :], vec)
        wanted.append(vec)
    wanted = jnp.concatenate(wanted, axis=1)
    slot_ids = lax.broadcasted_iota(jnp.int32, (bnd_ref.shape[0], n_d * send), 0)
    owner = jnp.sum(jnp.where(slot_ids == wanted, bnd_ref[...], 0), axis=0, keepdims=True)
    own_ids = lax.broadcasted_iota(jnp.int32, (rows, n_d * send), 0)
    pick_t32 = jnp.where(own_ids == owner, 1.0, 0.0)
    pick_t = pick_t32.astype(BF16)
    pick = pick_t32.T.astype(BF16)

    out1[...] = dot_nn(pick, h_ref[...]).astype(BF16)
    exchange_start(1, out1, ghost1, send)

    h32 = h_ref[...].astype(F32)
    h_t32 = h32.T
    h_t = h_t32.astype(BF16)

    def rel_tile(layer, lo, count):
        part = rel_e[pl.ds(layer * feat, feat), pl.ds(lo, count)].astype(F32)
        return jnp.concatenate([part] * queries, axis=0)

    def aggregate(layer, table_t, onehot, save, lo, count):
        sourced = dot_nn(table_t, onehot[...])
        save[:, pl.ds(lo, count)] = sourced.astype(BF16)
        message = split_hi_lo(sourced * rel_tile(layer, lo, count), 0)
        both = dot_nt(message, vt[:, pl.ds(lo, count)])
        return both[:wide] + both[wide:]

    def normalise(summed, w_ref):
        summed_b = summed.astype(BF16)
        normed, rstds = [], []
        for q in range(queries):
            mixed = lax.dot_general(
                w_ref[...],
                summed_b[q * feat : (q + 1) * feat],
                (((0,), (0,)), ((), ())),
                preferred_element_type=F32,
            )
            center = mixed - jnp.mean(mixed, axis=0, keepdims=True)
            rstd = lax.rsqrt(jnp.mean(center * center, axis=0, keepdims=True) + 1e-05)
            normed.append(center * rstd)
            rstds.append(rstd)
        return summed_b, normed, rstds

    def back_layer(up_t, normed, rstds, summed_b, w_ref):
        wgrad = jnp.zeros((feat, feat), F32)
        dsum = []
        for q in range(queries):
            y = normed[q]
            sig = jax.nn.sigmoid(y)
            dact = up_t[q * feat : (q + 1) * feat] * sig * (1.0 + y * (1.0 - sig))
            dmix = rstds[q] * (
                dact
                - jnp.mean(dact, axis=0, keepdims=True)
                - y * jnp.mean(dact * y, axis=0, keepdims=True)
            )
            dmix_b = dmix.astype(BF16)
            wgrad = wgrad + dot_nt(summed_b[q * feat : (q + 1) * feat], dmix_b)
            dsum.append(dot_nn(w_ref[...], dmix_b).astype(BF16))
        return wgrad, jnp.concatenate(dsum, axis=0)

    def rel_grad(down, save):
        prod = down * save[...].astype(F32)
        tot = prod[:feat]
        for q in range(1, queries):
            tot = tot + prod[q * feat : (q + 1) * feat]
        both = dot_nt(rt[pl.ds(0, rel_rows), :], split_hi_lo(tot, 0))
        return both[:, :feat] + both[:, feat:]

    def table_grad(layer, down, onehot, lo, count):
        message = split_hi_lo(down[:, lo : lo + count] * rel_tile(layer, lo, count), 0)
        both = dot_nt(onehot[...], message)
        return both[:, :wide] + both[:, wide:]

    def give_back(ret_in):
        both = dot_nn(pick_t, split_hi_lo(ret_in[...], 1))
        return both[:, :wide] + both[:, wide:]

    sum1 = aggregate(0, h_t, st_in, x1, 0, e_in) + boost
    exchange_wait(1, out1, ghost1, send)
    sum1 = sum1 + aggregate(0, ghost1[...].astype(F32).T.astype(BF16), st_bd, x1, e_in, e_bd)
    sum1_b, norm1, rstd1 = normalise(sum1, w1_ref)
    h2_t = (
        jnp.concatenate([y * jax.nn.sigmoid(y) for y in norm1], axis=0) + h_t32
    ).astype(BF16)

    out2[...] = dot_nt(pick, h2_t).astype(BF16)
    exchange_start(2, out2, ghost2, send)
    sum2 = aggregate(1, h2_t, st_in, x2, 0, e_in) + boost
    exchange_wait(2, out2, ghost2, send)
    sum2 = sum2 + aggregate(1, ghost2[...].astype(F32).T.astype(BF16), st_bd, x2, e_in, e_bd)
    sum2_b, norm2, rstd2 = normalise(sum2, w2_ref)

    cot32 = cot_ref[...].astype(F32)
    wg2, dsum2 = back_layer(cot32.T, norm2, rstd2, sum2_b, w2_ref)
    down2 = dot_nn(dsum2, vt[...])
    ret_out2[...] = table_grad(1, down2, st_bd, e_in, e_bd)
    exchange_start(3, ret_out2, ret_in2, send)
    mid = cot32 + table_grad(1, down2, st_in, 0, e_in)
    pack(1, rel_grad(down2, x2), wg2)
    exchange_wait(3, ret_out2, ret_in2, send)
    rs_start(1)
    mid = mid + give_back(ret_in2)

    wg1, dsum1 = back_layer(mid.T, norm1, rstd1, sum1_b, w1_ref)
    down1 = dot_nn(dsum1, vt[...])
    rs_finish_ag_start(1)
    pack(0, rel_grad(down1, x1), wg1)
    rs_start(0)
    ret_out1[...] = table_grad(0, down1, st_bd, e_in, e_bd)
    exchange_start(4, ret_out1, ret_in1, send)
    base = mid + table_grad(0, down1, st_in, 0, e_in)
    rs_finish_ag_start(0)
    exchange_wait(4, ret_out1, ret_in1, send)
    gin_ref[...] = base + give_back(ret_in1)
    ag_finish(1)
    unpack(1)
    ag_finish(0)
    unpack(0)


def body(
    h_in,
    cotangent,
    w_one,
    w_two,
    rel_one,
    rel_two,
    query_emb,
    q_head,
    q_rel,
    bnd_rows,
    ghost_slots,
    edges_in,
    edges_bd,
):
    rows, wide = h_in.shape
    feat = w_one.shape[0]
    queries = wide // feat
    rel_count = rel_one.shape[0]
    n_d = lax.axis_size("dom")
    n_q = lax.axis_size("query")
    total = n_d * n_q
    send = ghost_slots.shape[1]
    ghosts = n_d * send
    e_in, e_bd = edges_in.shape[1], edges_bd.shape[1]
    edges = e_in + e_bd
    rel_pad = -(-(rel_count + 1) // 128) * 128
    rel_rows = -(-(rel_count + 1) // 16) * 16
    half = -(-((rel_rows + feat + 1) // 2) // CHUNK) * CHUNK
    n_chunks = half // CHUNK
    scale_w = 1.0 / math.sqrt(rows * n_d * queries * n_q)
    scale_r = math.sqrt(rel_count / (n_d * edges * queries * n_q))

    tables = jnp.concatenate([rel_one, rel_two, query_emb], axis=1)
    rel_t = jnp.pad(tables, ((0, rel_pad - rel_count), (0, 0))).T
    slots = jnp.broadcast_to(jnp.tile(ghost_slots, (1, 128 // send))[:, None, :], (n_d, 8, 128))

    vmem = pl.BlockSpec(memory_space=pltpu.VMEM)
    smem = pl.BlockSpec(memory_space=pltpu.SMEM)
    dma = pltpu.SemaphoreType.DMA
    return pl.pallas_call(
        functools.partial(kernel, n_q, n_d, scale_w, scale_r, rel_count, rel_rows),
        out_shape=(
            jax.ShapeDtypeStruct((rows, wide), F32),
            jax.ShapeDtypeStruct((2, feat, feat), F32),
            jax.ShapeDtypeStruct((2, rel_count, feat), F32),
        ),
        in_specs=[vmem] * 5 + [smem] * 2 + [vmem] * 4,
        out_specs=(vmem, vmem, vmem),
        scratch_shapes=[
            pltpu.VMEM((rel_pad, edges), BF16),
            pltpu.VMEM((rows, edges), BF16),
            pltpu.VMEM((rows, e_in), BF16),
            pltpu.VMEM((ghosts, e_bd), BF16),
            pltpu.VMEM((2 * feat, edges), BF16),
            pltpu.VMEM((wide, edges), BF16),
            pltpu.VMEM((wide, edges), BF16),
            pltpu.VMEM((n_d, 8, 128), jnp.int32),
            pltpu.VMEM((ghosts, wide), BF16),
            pltpu.VMEM((ghosts, wide), BF16),
            pltpu.VMEM((ghosts, wide), BF16),
            pltpu.VMEM((ghosts, wide), BF16),
            pltpu.VMEM((ghosts, wide), F32),
            pltpu.VMEM((ghosts, wide), F32),
            pltpu.VMEM((ghosts, wide), F32),
            pltpu.VMEM((ghosts, wide), F32),
            pltpu.VMEM((2, half, 2 * feat), F32),
            pltpu.VMEM((2, total, CHUNK, 2 * feat), F32),
            pltpu.VMEM((2, CHUNK, 2 * feat), F32),
            pltpu.VMEM((2, half, 2 * feat), F32),
            dma((5, n_d)),
            dma((5, n_d)),
            dma((2, n_chunks)),
            dma((2, total)),
            dma((2, total)),
            dma((2, n_chunks)),
        ],
        compiler_params=pltpu.CompilerParams(
            collective_id=0, has_side_effects=True, vmem_limit_bytes=48 * 1024 * 1024
        ),
    )(
        h_in,
        cotangent,
        w_one,
        w_two,
        rel_t,
        q_head,
        q_rel,
        bnd_rows[:, None],
        slots,
        edges_in,
        edges_bd,
    )


def solution(mesh):
    return jax.shard_map(
        body,
        mesh=mesh,
        in_specs=(
            P("dom", "query"),
            P("dom", "query"),
            P(),
            P(),
            P(),
            P(),
            P(),
            P("query"),
            P("query"),
            P("dom"),
            P("dom", None),
            P(None, "dom"),
            P(None, "dom"),
        ),
        out_specs=(P("dom", "query"), P(), P()),
        check_vma=False,
    )
```

```python
import functools
import math

import jax
import jax.numpy as jnp
from jax import lax
from jax.experimental import pallas as pl
from jax.experimental.pallas import tpu as pltpu
from jax.sharding import PartitionSpec as P

MESH = pl.DeviceIdType.MESH
F32 = jnp.float32
BF16 = jnp.bfloat16
CHUNK = 16


def dot_nn(a, b):
    return lax.dot_general(a, b, (((1,), (0,)), ((), ())), preferred_element_type=F32)


def dot_nt(a, b):
    return lax.dot_general(a, b, (((1,), (1,)), ((), ())), preferred_element_type=F32)


def split_hi_lo(x, axis):
    hi = x.astype(BF16)
    lo = (x - hi.astype(F32)).astype(BF16)
    return jnp.concatenate([hi, lo], axis=axis)


def onehot_into(dest, ids, col0, block):
    rows = dest.shape[0]
    count = ids.shape[1]

    def fill(i, carry):
        base = pl.multiple_of(i * block, block)
        row_ids = lax.broadcasted_iota(jnp.int32, (block, count), 0) + base
        dest[pl.ds(base, block), pl.ds(col0, count)] = jnp.where(row_ids == ids, 1.0, 0.0).astype(BF16)
        return carry

    lax.fori_loop(0, rows // block, fill, 0)


def kernel(
    n_q,
    n_d,
    scale_w,
    scale_r,
    rel_count,
    rel_rows,
    h_ref,
    cot_ref,
    w1_ref,
    w2_ref,
    r1_ref,
    r2_ref,
    qe_ref,
    qhead_ref,
    qrel_ref,
    bnd_ref,
    gs_ref,
    ein_ref,
    ebd_ref,
    gin_ref,
    gw_ref,
    grel_ref,
    relt,
    gs_x,
    rt,
    vt,
    st_in,
    st_bd,
    rel_e,
    x1,
    x2,
    req,
    out1,
    ghost1,
    out2,
    ghost2,
    ret_out2,
    ret_in2,
    ret_out1,
    ret_in1,
    red_src,
    red_in,
    red_sum,
    red_all,
    xsend,
    xrecv,
    rsend,
    rrecv,
    gsend,
    grecv,
):
    me_d = lax.axis_index("dom")
    me_q = lax.axis_index("query")
    total = n_q * n_d
    lin = me_q * n_d + me_d
    feat = w1_ref.shape[0]
    rows, wide = h_ref.shape
    queries = wide // feat
    send = ghost1.shape[0] // n_d
    e_in = ein_ref.shape[1]
    e_bd = ebd_ref.shape[1]
    lanes = red_all.shape[2] // 128
    n_chunks = feat // CHUNK * lanes

    def tile_of(c):
        return (
            pl.ds(pl.multiple_of(c // lanes * CHUNK, CHUNK), CHUNK),
            pl.ds(pl.multiple_of(lax.rem(c, lanes) * 128, 128), 128),
        )

    barrier = pltpu.get_barrier_semaphore()

    def greet(i, carry):
        t = lax.rem(lin + i, total)
        pl.semaphore_signal(
            barrier, inc=1, device_id=(t // n_d, lax.rem(t, n_d)), device_id_type=MESH
        )
        return carry

    lax.fori_loop(1, total, greet, 0)

    def block_copy(phase, src, dst, size, i, send_to):
        peer = lax.rem(me_d + i, n_d)
        del send_to
        if size is None:
            s, d = src.at[peer], dst.at[me_d]
        else:
            s = src.at[pl.ds(pl.multiple_of(peer * size, size), size)]
            d = dst.at[pl.ds(pl.multiple_of(me_d * size, size), size)]
        return pltpu.make_async_remote_copy(
            src_ref=s,
            dst_ref=d,
            send_sem=xsend.at[phase, i],
            recv_sem=xrecv.at[phase, i],
            device_id=(me_q, peer),
            device_id_type=MESH,
        )

    def exchange_start(phase, src, dst, size):
        def go(i, carry):
            block_copy(phase, src, dst, size, i, True).start()
            return carry

        lax.fori_loop(1, n_d, go, 0)
        if size is None:
            dst[me_d] = src[me_d]
        else:
            own = pl.ds(pl.multiple_of(me_d * size, size), size)
            dst[own, :] = src[own, :]

    def exchange_wait(phase, src, dst, size):
        def go(i, carry):
            block_copy(phase, src, dst, size, i, False).wait()
            return carry

        lax.fori_loop(1, n_d, go, 0)

    mine = (lin * n_chunks + total - 1) // total
    adds = jnp.logical_and(mine < n_chunks, (mine * total) // n_chunks == lin)

    def rs_copy(layer, c):
        t = (c * total) // n_chunks
        return t, pltpu.make_async_remote_copy(
            src_ref=red_src.at[(layer, *tile_of(c))],
            dst_ref=red_in.at[layer, lin],
            send_sem=rsend.at[layer, c],
            recv_sem=rrecv.at[layer, lin],
            device_id=(t // n_d, lax.rem(t, n_d)),
            device_id_type=MESH,
        )

    def rs_start(layer):
        def go(c, carry):
            t, copy = rs_copy(layer, c)

            @pl.when(t != lin)
            def _():
                copy.start()

            return carry

        lax.fori_loop(0, n_chunks, go, 0)

    def ag_copy(layer, c, i):
        t = lax.rem(lin + i, total)
        return pltpu.make_async_remote_copy(
            src_ref=red_sum.at[layer],
            dst_ref=red_all.at[(layer, *tile_of(c))],
            send_sem=gsend.at[layer, i],
            recv_sem=grecv.at[layer, c],
            device_id=(t // n_d, lax.rem(t, n_d)),
            device_id_type=MESH,
        )

    def rs_finish_ag_start(layer):
        @pl.when(adds)
        def _():
            def take(i, acc):
                s = lax.rem(lin + i, total)
                pltpu.make_async_remote_copy(
                    src_ref=red_src.at[(layer, *tile_of(0))],
                    dst_ref=red_in.at[layer, s],
                    send_sem=rsend.at[layer, 0],
                    recv_sem=rrecv.at[layer, s],
                    device_id=(s // n_d, lax.rem(s, n_d)),
                    device_id_type=MESH,
                ).wait_recv()
                return acc + red_in[layer, s].astype(F32)

            own = red_src[(layer, *tile_of(mine))].astype(F32)
            acc = lax.fori_loop(1, total, take, own).astype(BF16)
            red_sum[layer] = acc
            red_all[(layer, *tile_of(mine))] = acc

            def put(i, carry):
                ag_copy(layer, mine, i).start()
                return carry

            lax.fori_loop(1, total, put, 0)

    def ag_finish(layer):
        def each(c, carry):
            t, copy = rs_copy(layer, c)

            @pl.when(t != lin)
            def _():
                copy.wait_send()
                ag_copy(layer, c, 1).wait_recv()

            return carry

        lax.fori_loop(0, n_chunks, each, 0)

        @pl.when(adds)
        def _():
            def done(i, carry):
                ag_copy(layer, mine, i).wait_send()
                return carry

            lax.fori_loop(1, total, done, 0)

    def pack(layer, rg, wg):
        parts = [rg, wg]
        left = lanes * 128 - rel_rows - feat
        if left:
            parts.append(jnp.zeros((feat, left), F32))
        red_src[layer] = jnp.concatenate(parts, axis=1).astype(BF16)

    def unpack(layer):
        summed = red_all[layer].astype(F32)
        grel_ref[layer] = summed[:, :rel_count] * scale_r
        gw_ref[layer] = summed[:, rel_rows : rel_rows + feat] * scale_w

    per = 128 // send
    spread = jnp.concatenate([gs_ref[...]] * per, axis=1)
    for p in range(n_d):
        gs_x[p] = spread[p : p + 1, :]

    onehot_into(vt, ein_ref[1:2, :], 0, 64)
    onehot_into(vt, ebd_ref[1:2, :], e_in, 64)
    pl.semaphore_wait(barrier, total - 1)
    exchange_start(0, gs_x, req, None)
    onehot_into(st_in, ein_ref[0:1, :], 0, 64)
    onehot_into(st_bd, ebd_ref[0:1, :], 0, 64)
    onehot_into(rt, ein_ref[2:3, :], 0, 32)
    onehot_into(rt, ebd_ref[2:3, :], e_in, 32)
    relt[...] = jnp.zeros_like(relt)
    relt[pl.ds(0, feat), pl.ds(0, rel_count)] = r1_ref[...]
    relt[pl.ds(feat, feat), pl.ds(0, rel_count)] = r2_ref[...]
    rel_e[...] = dot_nn(relt[...], rt[...]).astype(BF16)

    row_ids = lax.broadcasted_iota(jnp.int32, (feat, rows), 1) + me_d * rows
    lane_rel = lax.broadcasted_iota(jnp.int32, (feat, rel_count), 1)
    qtab = qe_ref[...].astype(F32)
    boost_parts = []
    for q in range(queries):
        vec = jnp.sum(jnp.where(lane_rel == qrel_ref[q], qtab, 0.0), axis=1, keepdims=True)
        boost_parts.append(jnp.where(row_ids == qhead_ref[q], vec, 0.0))
    boost = jnp.concatenate(boost_parts, axis=0)

    exchange_wait(0, gs_x, req, None)
    lane_group = lax.broadcasted_iota(jnp.int32, (1, 128), 1) // send
    wanted = []
    for j in range(n_d // per):
        vec = jnp.zeros((1, 128), jnp.int32)
        for k in range(per):
            vec = jnp.where(lane_group == k, req[j * per + k, 0:1, :], vec)
        wanted.append(vec)
    wanted = jnp.concatenate(wanted, axis=1)
    slots = bnd_ref.shape[1]
    slot_ids = lax.broadcasted_iota(jnp.int32, (slots, n_d * send), 0)
    own_ids = lax.broadcasted_iota(jnp.int32, (rows, slots), 0)
    row_of = jnp.where(own_ids == bnd_ref[...], 1.0, 0.0).astype(BF16)
    pick_t32 = dot_nn(row_of, jnp.where(slot_ids == wanted, 1.0, 0.0).astype(BF16))
    pick_t = pick_t32.astype(BF16)
    pick = pick_t32.T.astype(BF16)

    out1[...] = dot_nn(pick, h_ref[...]).astype(BF16)
    exchange_start(1, out1, ghost1, send)

    h32 = h_ref[...].astype(F32)
    h_t32 = h32.T
    h_t = h_t32.astype(BF16)

    def rel_tile(layer, lo, count):
        part = rel_e[pl.ds(layer * feat, feat), pl.ds(lo, count)].astype(F32)
        return jnp.concatenate([part] * queries, axis=0)

    def aggregate(layer, table_t, onehot, save, lo, count):
        sourced = dot_nn(table_t, onehot[...])
        save[:, pl.ds(lo, count)] = sourced.astype(BF16)
        message = split_hi_lo(sourced * rel_tile(layer, lo, count), 0)
        both = dot_nt(message, vt[:, pl.ds(lo, count)])
        return both[:wide] + both[wide:]

    def normalise(summed, w_ref):
        summed_b = summed.astype(BF16)
        normed, rstds = [], []
        for q in range(queries):
            mixed = lax.dot_general(
                w_ref[...],
                summed_b[q * feat : (q + 1) * feat],
                (((0,), (0,)), ((), ())),
                preferred_element_type=F32,
            )
            center = mixed - jnp.mean(mixed, axis=0, keepdims=True)
            rstd = lax.rsqrt(jnp.mean(center * center, axis=0, keepdims=True) + 1e-05)
            normed.append(center * rstd)
            rstds.append(rstd)
        return summed_b, normed, rstds

    def back_layer(up_t, normed, rstds, summed_b, w_ref):
        wgrad = jnp.zeros((feat, feat), F32)
        dsum = []
        for q in range(queries):
            y = normed[q]
            sig = jax.nn.sigmoid(y)
            dact = up_t[q * feat : (q + 1) * feat] * sig * (1.0 + y * (1.0 - sig))
            dmix = rstds[q] * (
                dact
                - jnp.mean(dact, axis=0, keepdims=True)
                - y * jnp.mean(dact * y, axis=0, keepdims=True)
            )
            dmix_b = dmix.astype(BF16)
            wgrad = wgrad + dot_nt(summed_b[q * feat : (q + 1) * feat], dmix_b)
            dsum.append(dot_nn(w_ref[...], dmix_b).astype(BF16))
        return wgrad, jnp.concatenate(dsum, axis=0)

    def rel_grad(down, save):
        prod = down * save[...].astype(F32)
        tot = prod[:feat]
        for q in range(1, queries):
            tot = tot + prod[q * feat : (q + 1) * feat]
        both = dot_nt(split_hi_lo(tot, 0), rt[pl.ds(0, rel_rows), :])
        return both[:feat] + both[feat:]

    def table_grad(layer, down, onehot, lo, count):
        message = split_hi_lo(down[:, lo : lo + count] * rel_tile(layer, lo, count), 0)
        both = dot_nt(onehot[...], message)
        return both[:, :wide] + both[:, wide:]

    def give_back(ret_in):
        return dot_nn(pick_t, ret_in[...])

    sum1 = aggregate(0, h_t, st_in, x1, 0, e_in) + boost
    exchange_wait(1, out1, ghost1, send)
    sum1 = sum1 + aggregate(0, ghost1[...].astype(F32).T.astype(BF16), st_bd, x1, e_in, e_bd)
    sum1_b, norm1, rstd1 = normalise(sum1, w1_ref)
    h2_t = (
        jnp.concatenate([y * jax.nn.sigmoid(y) for y in norm1], axis=0) + h_t32
    ).astype(BF16)

    out2[...] = dot_nt(pick, h2_t).astype(BF16)
    exchange_start(2, out2, ghost2, send)
    sum2 = aggregate(1, h2_t, st_in, x2, 0, e_in) + boost
    exchange_wait(2, out2, ghost2, send)
    sum2 = sum2 + aggregate(1, ghost2[...].astype(F32).T.astype(BF16), st_bd, x2, e_in, e_bd)
    sum2_b, norm2, rstd2 = normalise(sum2, w2_ref)

    cot32 = cot_ref[...].astype(F32)
    wg2, dsum2 = back_layer(cot32.T, norm2, rstd2, sum2_b, w2_ref)
    down2 = dot_nn(dsum2, vt[...])
    ret_out2[...] = table_grad(1, down2, st_bd, e_in, e_bd).astype(BF16)
    exchange_start(3, ret_out2, ret_in2, send)
    mid = cot32 + table_grad(1, down2, st_in, 0, e_in)
    pack(1, rel_grad(down2, x2), wg2)
    exchange_wait(3, ret_out2, ret_in2, send)
    rs_start(1)
    mid = mid + give_back(ret_in2)

    wg1, dsum1 = back_layer(mid.T, norm1, rstd1, sum1_b, w1_ref)
    down1 = dot_nn(dsum1, vt[...])
    pack(0, rel_grad(down1, x1), wg1)
    rs_start(0)
    ret_out1[...] = table_grad(0, down1, st_bd, e_in, e_bd).astype(BF16)
    exchange_start(4, ret_out1, ret_in1, send)
    rs_finish_ag_start(1)
    base = mid + table_grad(0, down1, st_in, 0, e_in)
    rs_finish_ag_start(0)
    exchange_wait(4, ret_out1, ret_in1, send)
    gin_ref[...] = base + give_back(ret_in1)
    ag_finish(1)
    unpack(1)
    ag_finish(0)
    unpack(0)


def body(
    h_in,
    cotangent,
    w_one,
    w_two,
    rel_one,
    rel_two,
    query_emb,
    q_head,
    q_rel,
    bnd_rows,
    ghost_slots,
    edges_in,
    edges_bd,
):
    rows, wide = h_in.shape
    feat = w_one.shape[0]
    queries = wide // feat
    rel_count = rel_one.shape[0]
    n_d = lax.axis_size("dom")
    n_q = lax.axis_size("query")
    total = n_d * n_q
    send = ghost_slots.shape[1]
    ghosts = n_d * send
    e_in, e_bd = edges_in.shape[1], edges_bd.shape[1]
    edges = e_in + e_bd
    rel_pad = -(-(rel_count + 1) // 128) * 128
    rel_rows = -(-(rel_count + 1) // 16) * 16
    width = -(-(rel_rows + feat) // 128) * 128
    n_chunks = feat // CHUNK * (width // 128)
    scale_w = 1.0 / math.sqrt(rows * n_d * queries * n_q)
    scale_r = math.sqrt(rel_count / (n_d * edges * queries * n_q))

    vmem = pl.BlockSpec(memory_space=pltpu.VMEM)
    smem = pl.BlockSpec(memory_space=pltpu.SMEM)
    dma = pltpu.SemaphoreType.DMA
    grad_in, grad_w, grad_rel_t = pl.pallas_call(
        functools.partial(kernel, n_q, n_d, scale_w, scale_r, rel_count, rel_rows),
        out_shape=(
            jax.ShapeDtypeStruct((rows, wide), F32),
            jax.ShapeDtypeStruct((2, feat, feat), F32),
            jax.ShapeDtypeStruct((2, feat, rel_count), F32),
        ),
        in_specs=[vmem] * 7 + [smem] * 2 + [vmem] * 4,
        out_specs=(vmem, vmem, vmem),
        scratch_shapes=[
            pltpu.VMEM((2 * feat, rel_pad), BF16),
            pltpu.VMEM((n_d, 1, 128), jnp.int32),
            pltpu.VMEM((rel_pad, edges), BF16),
            pltpu.VMEM((rows, edges), BF16),
            pltpu.VMEM((rows, e_in), BF16),
            pltpu.VMEM((ghosts, e_bd), BF16),
            pltpu.VMEM((2 * feat, edges), BF16),
            pltpu.VMEM((wide, edges), BF16),
            pltpu.VMEM((wide, edges), BF16),
            pltpu.VMEM((n_d, 1, 128), jnp.int32),
            pltpu.VMEM((ghosts, wide), BF16),
            pltpu.VMEM((ghosts, wide), BF16),
            pltpu.VMEM((ghosts, wide), BF16),
            pltpu.VMEM((ghosts, wide), BF16),
            pltpu.VMEM((ghosts, wide), BF16),
            pltpu.VMEM((ghosts, wide), BF16),
            pltpu.VMEM((ghosts, wide), BF16),
            pltpu.VMEM((ghosts, wide), BF16),
            pltpu.VMEM((2, feat, width), BF16),
            pltpu.VMEM((2, total, CHUNK, 128), BF16),
            pltpu.VMEM((2, CHUNK, 128), BF16),
            pltpu.VMEM((2, feat, width), BF16),
            dma((5, n_d)),
            dma((5, n_d)),
            dma((2, n_chunks)),
            dma((2, total)),
            dma((2, total)),
            dma((2, n_chunks)),
        ],
        compiler_params=pltpu.CompilerParams(
            collective_id=0, has_side_effects=True, vmem_limit_bytes=48 * 1024 * 1024
        ),
    )(
        h_in,
        cotangent,
        w_one,
        w_two,
        rel_one.T,
        rel_two.T,
        query_emb.T,
        q_head,
        q_rel,
        bnd_rows[None, :],
        ghost_slots,
        edges_in,
        edges_bd,
    )
    return grad_in, grad_w, jnp.swapaxes(grad_rel_t, 1, 2)


def solution(mesh):
    return jax.shard_map(
        body,
        mesh=mesh,
        in_specs=(
            P("dom", "query"),
            P("dom", "query"),
            P(),
            P(),
            P(),
            P(),
            P(),
            P("query"),
            P("query"),
            P("dom"),
            P("dom", None),
            P(None, "dom"),
            P(None, "dom"),
        ),
        out_specs=(P("dom", "query"), P(), P()),
        check_vma=False,
    )
```

```python
import functools
import math

import jax
import jax.numpy as jnp
from jax import lax
from jax.experimental import pallas as pl
from jax.experimental.pallas import tpu as pltpu
from jax.sharding import PartitionSpec as P

MESH = pl.DeviceIdType.MESH
F32 = jnp.float32
BF16 = jnp.bfloat16
CHUNK = 16


def dot_nn(a, b):
    return lax.dot_general(a, b, (((1,), (0,)), ((), ())), preferred_element_type=F32)


def dot_nt(a, b):
    return lax.dot_general(a, b, (((1,), (1,)), ((), ())), preferred_element_type=F32)


def split_hi_lo(x, axis):
    hi = x.astype(BF16)
    lo = (x - hi.astype(F32)).astype(BF16)
    return jnp.concatenate([hi, lo], axis=axis)


def onehot_into(dest, ids, col0, block):
    rows = dest.shape[0]
    count = ids.shape[1]

    def fill(i, carry):
        base = pl.multiple_of(i * block, block)
        row_ids = lax.broadcasted_iota(jnp.int32, (block, count), 0) + base
        dest[pl.ds(base, block), pl.ds(col0, count)] = jnp.where(row_ids == ids, 1.0, 0.0).astype(BF16)
        return carry

    lax.fori_loop(0, rows // block, fill, 0)


def loop(low, high, step):
    if high - low <= 32:
        for i in range(low, high):
            step(i, 0)
    else:
        lax.fori_loop(low, high, step, 0)


def div(a, b):
    return a // b if isinstance(a, int) else lax.div(a, b)


def rem(a, b):
    return a % b if isinstance(a, int) else lax.rem(a, b)


def aligned(a, b):
    return a if isinstance(a, int) else pl.multiple_of(a, b)


def kernel(
    n_q,
    n_d,
    scale_w,
    scale_r,
    rel_count,
    rel_rows,
    *refs,
):
    n_in = 13
    hbm = refs[:n_in]
    gin_ref, gw_ref, grel_ref = refs[n_in : n_in + 3]
    local = refs[n_in + 3 : 2 * n_in + 3]
    (
        h_ref, cot_ref, w1_ref, w2_ref, r1_ref, r2_ref, qe_ref, qhead_ref, qrel_ref, bnd_ref, gs_ref, ein_ref, ebd_ref,
    ) = local
    (
    relt,
    gs_x,
    rt,
    vt,
    st_in,
    st_bd,
    rel_e,
    x1,
    x2,
    req,
    out1,
    ghost1,
    out2,
    ghost2,
    ret_out2,
    ret_in2,
    ret_out1,
    ret_in1,
    red_src,
    red_in,
    red_sum,
    red_all,
    xsend,
    xrecv,
    rsend,
    rrecv,
    gsend,
    grecv,
    load_sem,
    ) = refs[2 * n_in + 3 :]
    me_d = lax.axis_index("dom")
    me_q = lax.axis_index("query")
    total = n_q * n_d
    lin = me_q * n_d + me_d
    feat = w1_ref.shape[0]
    rows, wide = h_ref.shape
    queries = wide // feat
    send = ghost1.shape[0] // n_d
    e_in = ein_ref.shape[1]
    e_bd = ebd_ref.shape[1]
    lanes = red_all.shape[2] // 128
    n_chunks = feat // CHUNK * lanes

    def tile_of(c):
        return (
            pl.ds(aligned(div(c, lanes) * CHUNK, CHUNK), CHUNK),
            pl.ds(aligned(rem(c, lanes) * 128, 128), 128),
        )

    barrier = pltpu.get_barrier_semaphore()

    def greet(i, carry):
        t = lax.rem(lin + i, total)
        pl.semaphore_signal(
            barrier, inc=1, device_id=(div(t, n_d), rem(t, n_d)), device_id_type=MESH
        )
        return carry

    loop(1, total, greet)
    loads = [
        pltpu.make_async_copy(src, dst, load_sem.at[k])
        for k, (src, dst) in enumerate(zip(hbm, local))
    ]
    for load in loads:
        load.start()
    for load in loads:
        load.wait()

    def block_copy(phase, src, dst, size, i, send_to):
        peer = lax.rem(me_d + i, n_d)
        del send_to
        if size is None:
            s, d = src.at[peer], dst.at[me_d]
        else:
            s = src.at[pl.ds(pl.multiple_of(peer * size, size), size)]
            d = dst.at[pl.ds(pl.multiple_of(me_d * size, size), size)]
        return pltpu.make_async_remote_copy(
            src_ref=s,
            dst_ref=d,
            send_sem=xsend.at[phase, i],
            recv_sem=xrecv.at[phase, i],
            device_id=(me_q, peer),
            device_id_type=MESH,
        )

    def exchange_start(phase, src, dst, size):
        def go(i, carry):
            block_copy(phase, src, dst, size, i, True).start()
            return carry

        loop(1, n_d, go)
        if size is None:
            dst[me_d] = src[me_d]
        else:
            own = pl.ds(pl.multiple_of(me_d * size, size), size)
            dst[own, :] = src[own, :]

    def exchange_wait(phase, src, dst, size):
        def go(i, carry):
            block_copy(phase, src, dst, size, i, False).wait()
            return carry

        loop(1, n_d, go)

    mine = (lin * n_chunks + total - 1) // total
    adds = jnp.logical_and(mine < n_chunks, (mine * total) // n_chunks == lin)

    def rs_copy(layer, c):
        t = div(c * total, n_chunks)
        return t, pltpu.make_async_remote_copy(
            src_ref=red_src.at[(layer, *tile_of(c))],
            dst_ref=red_in.at[layer, lin],
            send_sem=rsend.at[layer, c],
            recv_sem=rrecv.at[layer, lin],
            device_id=(div(t, n_d), rem(t, n_d)),
            device_id_type=MESH,
        )

    def rs_start(layer):
        def go(c, carry):
            t, copy = rs_copy(layer, c)

            @pl.when(t != lin)
            def _():
                copy.start()

            return carry

        loop(0, n_chunks, go)

    def ag_copy(layer, c, i):
        t = lax.rem(lin + i, total)
        return pltpu.make_async_remote_copy(
            src_ref=red_sum.at[layer],
            dst_ref=red_all.at[(layer, *tile_of(c))],
            send_sem=gsend.at[layer, i],
            recv_sem=grecv.at[layer, c],
            device_id=(div(t, n_d), rem(t, n_d)),
            device_id_type=MESH,
        )

    def rs_finish_ag_start(layer):
        @pl.when(adds)
        def _():
            def take(i, carry):
                s = lax.rem(lin + i, total)
                pltpu.make_async_remote_copy(
                    src_ref=red_src.at[(layer, *tile_of(0))],
                    dst_ref=red_in.at[layer, s],
                    send_sem=rsend.at[layer, 0],
                    recv_sem=rrecv.at[layer, s],
                    device_id=(div(s, n_d), rem(s, n_d)),
                    device_id_type=MESH,
                ).wait_recv()
                return carry

            loop(1, total, take)
            red_in[layer, lin] = red_src[(layer, *tile_of(mine))]
            acc = jnp.sum(red_in[layer].astype(F32), axis=0).astype(BF16)
            red_sum[layer] = acc
            red_all[(layer, *tile_of(mine))] = acc

            def put(i, carry):
                ag_copy(layer, mine, i).start()
                return carry

            loop(1, total, put)

    def ag_finish(layer):
        def each(c, carry):
            t, copy = rs_copy(layer, c)

            @pl.when(t != lin)
            def _():
                copy.wait_send()
                ag_copy(layer, c, 1).wait_recv()

            return carry

        loop(0, n_chunks, each)

        @pl.when(adds)
        def _():
            def done(i, carry):
                ag_copy(layer, mine, i).wait_send()
                return carry

            loop(1, total, done)

    def pack(layer, rg, wg):
        parts = [rg, wg]
        left = lanes * 128 - rel_rows - feat
        if left:
            parts.append(jnp.zeros((feat, left), F32))
        red_src[layer] = jnp.concatenate(parts, axis=1).astype(BF16)

    def unpack(layer):
        summed = red_all[layer].astype(F32)
        grel_ref[layer] = summed[:, :rel_count] * scale_r
        gw_ref[layer] = summed[:, rel_rows : rel_rows + feat] * scale_w

    per = 128 // send
    spread = jnp.concatenate([gs_ref[...]] * per, axis=1)
    for p in range(n_d):
        gs_x[p] = spread[p : p + 1, :]

    onehot_into(vt, ein_ref[1:2, :], 0, 64)
    onehot_into(vt, ebd_ref[1:2, :], e_in, 64)
    pl.semaphore_wait(barrier, total - 1)
    exchange_start(0, gs_x, req, None)
    onehot_into(st_in, ein_ref[0:1, :], 0, 64)
    onehot_into(st_bd, ebd_ref[0:1, :], 0, 64)
    onehot_into(rt, ein_ref[2:3, :], 0, 32)
    onehot_into(rt, ebd_ref[2:3, :], e_in, 32)
    relt[...] = jnp.zeros_like(relt)
    relt[pl.ds(0, feat), pl.ds(0, rel_count)] = r1_ref[...]
    relt[pl.ds(feat, feat), pl.ds(0, rel_count)] = r2_ref[...]
    rel_e[...] = dot_nn(relt[...], rt[...]).astype(BF16)

    row_ids = lax.broadcasted_iota(jnp.int32, (feat, rows), 1) + me_d * rows
    lane_rel = lax.broadcasted_iota(jnp.int32, (feat, rel_count), 1)
    qtab = qe_ref[...].astype(F32)
    boost_parts = []
    for q in range(queries):
        vec = jnp.sum(jnp.where(lane_rel == qrel_ref[q], qtab, 0.0), axis=1, keepdims=True)
        boost_parts.append(jnp.where(row_ids == qhead_ref[q], vec, 0.0))
    boost = jnp.concatenate(boost_parts, axis=0)

    exchange_wait(0, gs_x, req, None)
    lane_group = lax.broadcasted_iota(jnp.int32, (1, 128), 1) // send
    wanted = []
    for j in range(n_d // per):
        vec = jnp.zeros((1, 128), jnp.int32)
        for k in range(per):
            vec = jnp.where(lane_group == k, req[j * per + k, 0:1, :], vec)
        wanted.append(vec)
    wanted = jnp.concatenate(wanted, axis=1)
    slots = bnd_ref.shape[1]
    slot_ids = lax.broadcasted_iota(jnp.int32, (slots, n_d * send), 0)
    own_ids = lax.broadcasted_iota(jnp.int32, (rows, slots), 0)
    row_of = jnp.where(own_ids == bnd_ref[...], 1.0, 0.0).astype(BF16)
    pick_t32 = dot_nn(row_of, jnp.where(slot_ids == wanted, 1.0, 0.0).astype(BF16))
    pick_t = pick_t32.astype(BF16)
    pick = pick_t32.T.astype(BF16)

    out1[...] = dot_nn(pick, h_ref[...]).astype(BF16)
    exchange_start(1, out1, ghost1, send)

    h32 = h_ref[...].astype(F32)
    h_t32 = h32.T
    h_t = h_t32.astype(BF16)

    def rel_tile(layer, lo, count):
        part = rel_e[pl.ds(layer * feat, feat), pl.ds(lo, count)].astype(F32)
        return jnp.concatenate([part] * queries, axis=0)

    def aggregate(layer, table_t, onehot, save, lo, count):
        sourced = dot_nn(table_t, onehot[...])
        save[:, pl.ds(lo, count)] = sourced.astype(BF16)
        message = split_hi_lo(sourced * rel_tile(layer, lo, count), 0)
        both = dot_nt(message, vt[:, pl.ds(lo, count)])
        return both[:wide] + both[wide:]

    def normalise(summed, w_ref):
        summed_b = summed.astype(BF16)
        normed, rstds = [], []
        for q in range(queries):
            mixed = lax.dot_general(
                w_ref[...],
                summed_b[q * feat : (q + 1) * feat],
                (((0,), (0,)), ((), ())),
                preferred_element_type=F32,
            )
            center = mixed - jnp.mean(mixed, axis=0, keepdims=True)
            rstd = lax.rsqrt(jnp.mean(center * center, axis=0, keepdims=True) + 1e-05)
            normed.append(center * rstd)
            rstds.append(rstd)
        return summed_b, normed, rstds

    def back_layer(up_t, normed, rstds, summed_b, w_ref):
        wgrad = jnp.zeros((feat, feat), F32)
        dsum = []
        for q in range(queries):
            y = normed[q]
            sig = jax.nn.sigmoid(y)
            dact = up_t[q * feat : (q + 1) * feat] * sig * (1.0 + y * (1.0 - sig))
            dmix = rstds[q] * (
                dact
                - jnp.mean(dact, axis=0, keepdims=True)
                - y * jnp.mean(dact * y, axis=0, keepdims=True)
            )
            dmix_b = dmix.astype(BF16)
            wgrad = wgrad + dot_nt(summed_b[q * feat : (q + 1) * feat], dmix_b)
            dsum.append(dot_nn(w_ref[...], dmix_b).astype(BF16))
        return wgrad, jnp.concatenate(dsum, axis=0)

    def rel_grad(down, save):
        prod = down * save[...].astype(F32)
        tot = prod[:feat]
        for q in range(1, queries):
            tot = tot + prod[q * feat : (q + 1) * feat]
        both = dot_nt(split_hi_lo(tot, 0), rt[pl.ds(0, rel_rows), :])
        return both[:feat] + both[feat:]

    def table_grad(layer, down, onehot, lo, count):
        message = split_hi_lo(down[:, lo : lo + count] * rel_tile(layer, lo, count), 0)
        both = dot_nt(onehot[...], message)
        return both[:, :wide] + both[:, wide:]

    def give_back(ret_in):
        return dot_nn(pick_t, ret_in[...])

    sum1 = aggregate(0, h_t, st_in, x1, 0, e_in) + boost
    exchange_wait(1, out1, ghost1, send)
    sum1 = sum1 + aggregate(0, ghost1[...].astype(F32).T.astype(BF16), st_bd, x1, e_in, e_bd)
    sum1_b, norm1, rstd1 = normalise(sum1, w1_ref)
    h2_t = (
        jnp.concatenate([y * jax.nn.sigmoid(y) for y in norm1], axis=0) + h_t32
    ).astype(BF16)

    out2[...] = dot_nt(pick, h2_t).astype(BF16)
    exchange_start(2, out2, ghost2, send)
    sum2 = aggregate(1, h2_t, st_in, x2, 0, e_in) + boost
    exchange_wait(2, out2, ghost2, send)
    sum2 = sum2 + aggregate(1, ghost2[...].astype(F32).T.astype(BF16), st_bd, x2, e_in, e_bd)
    sum2_b, norm2, rstd2 = normalise(sum2, w2_ref)

    cot32 = cot_ref[...].astype(F32)
    wg2, dsum2 = back_layer(cot32.T, norm2, rstd2, sum2_b, w2_ref)
    down2 = dot_nn(dsum2, vt[...])
    ret_out2[...] = table_grad(1, down2, st_bd, e_in, e_bd).astype(BF16)
    exchange_start(3, ret_out2, ret_in2, send)
    mid = cot32 + table_grad(1, down2, st_in, 0, e_in)
    pack(1, rel_grad(down2, x2), wg2)
    exchange_wait(3, ret_out2, ret_in2, send)
    rs_start(1)
    mid = mid + give_back(ret_in2)

    wg1, dsum1 = back_layer(mid.T, norm1, rstd1, sum1_b, w1_ref)
    down1 = dot_nn(dsum1, vt[...])
    pack(0, rel_grad(down1, x1), wg1)
    rs_start(0)
    ret_out1[...] = table_grad(0, down1, st_bd, e_in, e_bd).astype(BF16)
    exchange_start(4, ret_out1, ret_in1, send)
    rs_finish_ag_start(1)
    base = mid + table_grad(0, down1, st_in, 0, e_in)
    rs_finish_ag_start(0)
    exchange_wait(4, ret_out1, ret_in1, send)
    gin_ref[...] = base + give_back(ret_in1)
    ag_finish(1)
    unpack(1)
    ag_finish(0)
    unpack(0)


def write_out(*refs):
    sems = refs[6]
    copies = [pltpu.make_async_copy(refs[k], refs[3 + k], sems.at[k]) for k in range(3)]
    for copy in copies:
        copy.start()
    for copy in copies:
        copy.wait()


def body(
    h_in,
    cotangent,
    w_one,
    w_two,
    rel_one,
    rel_two,
    query_emb,
    q_head,
    q_rel,
    bnd_rows,
    ghost_slots,
    edges_in,
    edges_bd,
):
    rows, wide = h_in.shape
    feat = w_one.shape[0]
    queries = wide // feat
    rel_count = rel_one.shape[0]
    n_d = lax.axis_size("dom")
    n_q = lax.axis_size("query")
    total = n_d * n_q
    send = ghost_slots.shape[1]
    ghosts = n_d * send
    e_in, e_bd = edges_in.shape[1], edges_bd.shape[1]
    edges = e_in + e_bd
    rel_pad = -(-(rel_count + 1) // 128) * 128
    rel_rows = -(-(rel_count + 1) // 16) * 16
    width = -(-(rel_rows + feat) // 128) * 128
    n_chunks = feat // CHUNK * (width // 128)
    scale_w = 1.0 / math.sqrt(rows * n_d * queries * n_q)
    scale_r = math.sqrt(rel_count / (n_d * edges * queries * n_q))

    args = (
        h_in,
        cotangent,
        w_one,
        w_two,
        rel_one.T,
        rel_two.T,
        query_emb.T,
        q_head,
        q_rel,
        bnd_rows[None, :],
        ghost_slots,
        edges_in,
        edges_bd,
    )
    spaces = [pltpu.VMEM] * 7 + [pltpu.SMEM] * 2 + [pltpu.VMEM] * 4

    vmem = pl.BlockSpec(memory_space=pltpu.VMEM)
    dma = pltpu.SemaphoreType.DMA
    grad_in, grad_w, grad_rel_t = pl.pallas_call(
        functools.partial(kernel, n_q, n_d, scale_w, scale_r, rel_count, rel_rows),
        out_shape=(
            jax.ShapeDtypeStruct((rows, wide), F32),
            jax.ShapeDtypeStruct((2, feat, feat), F32),
            jax.ShapeDtypeStruct((2, feat, rel_count), F32),
        ),
        in_specs=[pl.BlockSpec(memory_space=pltpu.HBM)] * len(args),
        out_specs=(vmem, vmem, vmem),
        scratch_shapes=[
            *(space(a.shape, a.dtype) for a, space in zip(args, spaces)),
            pltpu.VMEM((2 * feat, rel_pad), BF16),
            pltpu.VMEM((n_d, 1, 128), jnp.int32),
            pltpu.VMEM((rel_pad, edges), BF16),
            pltpu.VMEM((rows, edges), BF16),
            pltpu.VMEM((rows, e_in), BF16),
            pltpu.VMEM((ghosts, e_bd), BF16),
            pltpu.VMEM((2 * feat, edges), BF16),
            pltpu.VMEM((wide, edges), BF16),
            pltpu.VMEM((wide, edges), BF16),
            pltpu.VMEM((n_d, 1, 128), jnp.int32),
            pltpu.VMEM((ghosts, wide), BF16),
            pltpu.VMEM((ghosts, wide), BF16),
            pltpu.VMEM((ghosts, wide), BF16),
            pltpu.VMEM((ghosts, wide), BF16),
            pltpu.VMEM((ghosts, wide), BF16),
            pltpu.VMEM((ghosts, wide), BF16),
            pltpu.VMEM((ghosts, wide), BF16),
            pltpu.VMEM((ghosts, wide), BF16),
            pltpu.VMEM((2, feat, width), BF16),
            pltpu.VMEM((2, total, CHUNK, 128), BF16),
            pltpu.VMEM((2, CHUNK, 128), BF16),
            pltpu.VMEM((2, feat, width), BF16),
            dma((5, n_d)),
            dma((5, n_d)),
            dma((2, n_chunks)),
            dma((2, total)),
            dma((2, total)),
            dma((2, n_chunks)),
            dma((len(args),)),
        ],
        compiler_params=pltpu.CompilerParams(
            collective_id=0, has_side_effects=True, vmem_limit_bytes=48 * 1024 * 1024
        ),
    )(*args)
    grad_in, grad_w, grad_rel_t = pl.pallas_call(
        write_out,
        out_shape=tuple(jax.ShapeDtypeStruct(x.shape, x.dtype) for x in (grad_in, grad_w, grad_rel_t)),
        in_specs=[vmem] * 3,
        out_specs=[pl.BlockSpec(memory_space=pltpu.HBM)] * 3,
        scratch_shapes=[dma((3,))],
    )(grad_in, grad_w, grad_rel_t)
    return grad_in, grad_w, jnp.swapaxes(grad_rel_t, 1, 2)


def solution(mesh):
    return jax.shard_map(
        body,
        mesh=mesh,
        in_specs=(
            P("dom", "query"),
            P("dom", "query"),
            P(),
            P(),
            P(),
            P(),
            P(),
            P("query"),
            P("query"),
            P("dom"),
            P("dom", None),
            P(None, "dom"),
            P(None, "dom"),
        ),
        out_specs=(P("dom", "query"), P(), P()),
        check_vma=False,
    )
```
